512 devices in a mesh: row: 8 (over y), col: 64 (over z, x, core).
Axes of the slice: x: 4, y: 8, z: 8, core: 2. Of those that a mesh axis runs over, the one named last changes fastest.
Arguments:
- eigen_slab: float32 [8192, 65536], P('row', 'col'), may hold values from -6 to 6
- secular_poles: float32 [131072], P('col'), may hold values from 0 to 4, as said below
- coupling: float32 [131072], P('col'), may hold values from -7 to 7
- window_roots: float32 [128], replicated, may hold values from 0 to 4, as said below
- deflated: int32 [131072], P('col'), may hold values 0 or 1
- column_map: int32 [131072], P('col'), may hold values from 0 to 131071, as said below
Outputs:
- vectors: float32 [8192, 128], P(('row', 'col'))
The draws below stay inside these ranges and needn't reach their ends.
Inputs may be any that keep to these rules, and one draw needn't show every extreme that they name: `column_map`: A permutation of the 131072 columns. Grid column c holds columns c * 1024 to (c + 1) * 1024 - 1 and 65536 + c * 1024 to 65536 + (c + 1) * 1024 - 1 of the slab, and positions c * 2048 to (c + 1) * 2048 - 1. Of one grid column's positions, exactly 64 map to the columns of one grid column, 32 to each of 62 others, none to the remaining one. `secular_poles`: each pole lies between (k + 0.2) * 4 / 256 and (k + 0.8) * 4 / 256 for a whole number k. `window_roots`: each root lies within 0.15 * 4 / 256 of k * 4 / 256 for a whole number k of 1 to 255.
All inputs are finite; a program needn't handle non-finite values. No bound on the sum of `deflated` on one device may be relied on, other than what follows from the above.
Results may differ from the reference program's by a relative error of at most 0.0003.
Values sent between devices are 32-bit elements; how exact they have to be, the bound alone decides.
A program may use at most 64 MiB of HBM per device.

```python
import jax
import jax.numpy as jnp
from jax import lax

COLS_DEV = 1024
WIN = 128
HALF = 65536
ORDER = 131072
POS_DEV = 2048
ROWS = 8192
SLOTS = 256
SHARE = 32
CAP = 64


def draw_secular_poles(key, part):
    slot_key, spread_key = jax.random.split(jax.random.fold_in(key, 101), 2)
    slot_ids = jax.random.randint(slot_key, (ORDER,), 0, SLOTS).astype(jnp.float32)
    offset = jax.random.uniform(spread_key, (ORDER,), jnp.float32, -1.0, 1.0)
    return (slot_ids + 0.5 + 0.3 * offset) * (4.0 / SLOTS)


def draw_window_roots(key, part):
    slot_key, spread_key = jax.random.split(jax.random.fold_in(key, 202), 2)
    slot_ids = jax.random.randint(slot_key, (WIN,), 1, SLOTS).astype(jnp.float32)
    offset = jax.random.uniform(spread_key, (WIN,), jnp.float32, -0.15, 0.15)
    return (slot_ids + offset) * (4.0 / SLOTS)


def draw_coupling(key, part):
    value_key = jax.random.fold_in(key, 303)
    position = jnp.arange(ORDER, dtype=jnp.float32) / ORDER
    values = jax.random.truncated_normal(value_key, -4.0, 4.0, (ORDER,), jnp.float32)
    growth = 1.0 + 0.75 * position
    return values * growth


def draw_column_map(key, part):
    shift_key, source_key, target_key = jax.random.split(jax.random.fold_in(key, 404), 3)
    groups = ORDER // POS_DEV
    shifts = jax.random.permutation(shift_key, groups)[:groups - 1]
    slot_range = jnp.arange(POS_DEV, dtype=jnp.int32)
    group_of = jnp.where(slot_range < CAP, 0, 1 + (slot_range - CAP) // SHARE)
    source_order = jax.vmap(lambda sub_key: jax.random.permutation(sub_key, POS_DEV))(jax.random.split(source_key, groups))
    target_order = jax.vmap(lambda sub_key: jax.random.permutation(sub_key, POS_DEV))(jax.random.split(target_key, groups))
    source_dev = jnp.arange(groups, dtype=jnp.int32)[:, None]
    target_dev = (source_dev + shifts[group_of][None, :]) % groups
    local_target = target_order[target_dev, slot_range[None, :]]
    column = jnp.where(local_target < COLS_DEV, target_dev * COLS_DEV + local_target, HALF + target_dev * COLS_DEV + local_target - COLS_DEV)
    positions = source_dev * POS_DEV + source_order
    result = jnp.zeros((ORDER,), jnp.int32).at[positions.reshape(-1)].set(column.reshape(-1).astype(jnp.int32))
    return result.astype(jnp.int32)


def touch_ends(values, stream_key, low, high):
    extent = values.shape
    index_at = [jax.random.randint(jax.random.fold_in(stream_key, axis), (), 0, extent[axis]) for axis in range(len(extent))]
    values = values.at[tuple(index_at)].set(low)
    longest = extent.index(max(extent))
    index_at[longest] = (index_at[longest] + 1) % extent[longest]
    return values.at[tuple(index_at)].set(high)


def shard_levels(own_key, extent, shards, smallest, largest):
    def one(dim, blocks):
        steps = jax.random.uniform(jax.random.fold_in(jax.random.fold_in(own_key, 6), dim), (blocks,), jnp.float32, smallest / len(shards), largest / len(shards))
        return jnp.repeat(jnp.exp(steps), extent[dim] // blocks).reshape((-1,) + (1,) * (len(extent) - dim - 1))

    loudness = one(*shards[0])
    for cut in shards[1:]:
        loudness = loudness * one(*cut)
    return loudness


def bell_draw(rng, dims, deviation, limit, shards=(), kind=jnp.bfloat16):
    values = deviation * jax.random.normal(rng, dims, jnp.float32)
    if shards:
        values = values * shard_levels(rng, dims, shards, -0.22, 0.18)
    return jnp.clip(values, -limit, limit).astype(kind)


def setup_inputs(seed: int = 0) -> dict:
    seeds = jax.random.split(jax.random.key(seed), 7)
    return {
        "eigen_slab": bell_draw(seeds[0], (ROWS, HALF), 1.0, 6.0, ((0, 8), (1, 64)), jnp.float32),
        "secular_poles": draw_secular_poles(jax.random.fold_in(seeds[6], 71), 0),
        "coupling": draw_coupling(jax.random.fold_in(seeds[6], 71), 0),
        "window_roots": draw_window_roots(jax.random.fold_in(seeds[6], 71), 0),
        "deflated": touch_ends((jax.random.randint(seeds[4], (ORDER,), 0, 4) < 1).astype(jnp.int32), jax.random.fold_in(seeds[4], 1), 0, 1),
        "column_map": draw_column_map(jax.random.fold_in(seeds[6], 71), 0),
    }


def reference(eigen_slab, secular_poles, coupling, window_roots, deflated, column_map):
    distance = secular_poles[:, None] - window_roots[None, :]
    entries = jnp.where(deflated[:, None] == 0, coupling[:, None] / distance, jnp.zeros_like(distance))
    inverse = lax.rsqrt(lax.optimization_barrier(jnp.sum(entries * entries, axis=0)))
    scaled = entries * inverse[None, :]
    placed = jnp.zeros_like(scaled).at[column_map.astype(jnp.int32)].set(scaled)
    upper_part = jnp.dot(eigen_slab[:ROWS // 2], placed[:HALF], precision=lax.Precision.HIGHEST, preferred_element_type=jnp.float32)
    lower_part = jnp.dot(eigen_slab[ROWS // 2:], placed[HALF:], precision=lax.Precision.HIGHEST, preferred_element_type=jnp.float32)
    return jnp.concatenate([upper_part, lower_part], axis=0)
```

```python
import jax
import jax.numpy as jnp
from jax import lax
from jax.experimental import pallas as pl
from jax.experimental.pallas import tpu as pltpu
from jax.sharding import PartitionSpec as P

MESH = pl.DeviceIdType.MESH
BF = jnp.bfloat16
F32 = jnp.float32
NT = (((1,), (1,)), ((), ()))
HALF = 65536
ORDER_X = (2, 1, 3, 0)


def dot_nt(a, b):
    return lax.dot_general(a, b, NT, preferred_element_type=F32)


def split3(v):
    hi = v.astype(BF)
    rest = v - hi.astype(F32)
    mid = rest.astype(BF)
    low = (rest - mid.astype(F32)).astype(BF)
    return hi.astype(F32), mid.astype(F32), low.astype(F32)


def kernel(
    slab, poles_in, coup_in, roots_in, defl_in, cmap_in, out_ref,
    sf, sh, sl, poles, coup, roots, defl, cmap,
    pieces, hots, slots, outgoing, recv_a, send_b, recv_b,
    place_l, place_r, entry, prod, recv_c, send_x, recv_x, send_z, recv_z,
    in_sem, slab_sem, sa, ra, sb, rb, sc, rc, sx, rx, sz, rz,
):
    row = lax.axis_index("row")
    col = lax.axis_index("col")
    z = col // 8
    g = col % 8
    x = g // 2
    core = g % 2

    smalls = [
        pltpu.make_async_copy(s, d, in_sem.at[i])
        for i, (s, d) in enumerate(
            [(cmap_in, cmap), (poles_in, poles), (coup_in, coup), (defl_in, defl), (roots_in, roots)]
        )
    ]
    for c in smalls:
        c.start()
    slabs = [
        pltpu.make_async_copy(slab.at[:, i // 2, i % 2], sf.at[i], slab_sem.at[i]) for i in range(8)
    ]
    for c in slabs:
        c.start()

    barrier = pltpu.get_barrier_semaphore()
    for k in range(1, 8):
        pl.semaphore_signal(barrier, inc=1, device_id=(row, z * 8 + (g + k) % 8), device_id_type=MESH)
        pl.semaphore_signal(barrier, inc=1, device_id=(row, ((z + k) % 8) * 8 + g), device_id_type=MESH)

    for c in smalls:
        c.wait()

    cm = cmap[...]
    upper = (cm >= HALF).astype(jnp.int32)
    within = cm - upper * HALF
    target = within >> 10
    local = within & 1023
    order = (target & 7) * 8 + (target >> 3)
    order = jnp.where(upper == row // 4, order, -1)
    pole_v = poles[...]
    coup_v = jnp.where(defl[...] == 0, coup[...], 0.0)
    coup[...] = coup_v
    vals = (
        *split3(pole_v),
        *split3(coup_v),
        (local >> 7).astype(F32),
        (local & 127).astype(F32),
    )
    dest_id = lax.broadcasted_iota(jnp.int32, (64, 128), 0)
    slot_id = (lax.broadcasted_iota(jnp.int32, (128, 128), 0) & 63).astype(F32)
    for b in range(16):
        hots[pl.ds(64 * b, 64), :] = (order[b:b + 1, :] == dest_id).astype(F32).astype(BF)
    before = lax.broadcasted_iota(jnp.int32, (128, 256), 0)
    at = lax.broadcasted_iota(jnp.int32, (128, 256), 1)
    tri = ((before < at) | (at >= 128)).astype(F32).astype(BF)
    counts = jnp.dot(hots[...], tri, preferred_element_type=F32)
    carry = jnp.zeros((64, 128), F32)
    for b in range(16):
        lanes = pl.ds(128 * b, 128)
        hot = hots[pl.ds(64 * b, 64), :]
        block = counts[64 * b:64 * b + 64]
        rank = jnp.sum(hot.astype(F32) * (block[:, :128] + carry), axis=0, keepdims=True)
        carry = carry + block[:, 128:]
        slots[:, lanes] = (rank == slot_id).astype(F32).astype(BF)
        for i, v in enumerate(vals):
            pieces[pl.ds(64 * i, 64), lanes] = hot * jnp.broadcast_to(v[b:b + 1, :], (64, 128)).astype(BF)
    routed = dot_nt(pieces[...], slots[...])
    pole_o = (routed[0:64] + routed[64:128]) + routed[128:192]
    coup_o = (routed[192:256] + routed[256:320]) + routed[320:384]
    at_o = routed[384:448] * 128.0 + routed[448:512]
    low_lane = lax.broadcasted_iota(jnp.int32, (64, 128), 1) < 64
    outgoing[:, 0] = jnp.where(low_lane, pole_o, coup_o).reshape(8, 8, 128)
    outgoing[:, 1] = at_o.reshape(8, 8, 128)

    pl.semaphore_wait(barrier, 14)
    copies_a = []
    for k in range(1, 8):
        to = (g + k) % 8
        c = pltpu.make_async_remote_copy(
            src_ref=outgoing.at[to], dst_ref=recv_a.at[g], send_sem=sa.at[k], recv_sem=ra.at[k],
            device_id=(row, z * 8 + to), device_id_type=MESH,
        )
        c.start()
        copies_a.append(c)
    recv_a[g] = outgoing[g]

    roots_t = jnp.transpose(jnp.broadcast_to(roots[...], (128, 128)))
    sums = jnp.zeros((128, 128), F32)
    for b in range(16):
        e = coup_v[b:b + 1, :] / (pole_v[b:b + 1, :] - roots_t)
        sums = sums + e * e
    sums = jnp.sum(jnp.transpose(sums), axis=0, keepdims=True)
    lane1 = lax.broadcasted_iota(jnp.int32, (8, 128), 1)
    sub1 = lax.broadcasted_iota(jnp.int32, (8, 128), 0)
    sums8 = jnp.broadcast_to(sums, (8, 128))
    sums8 = jnp.where(sub1 == 0, pltpu.roll(sums8, 64, 1), sums8)

    for c in copies_a:
        c.wait_recv()
    for s in range(8):
        for k in range(2):
            send_b[pl.ds(k * 8 + s, 8, stride=16), :] = recv_a[s, k]
    for t in range(8):
        rows = pl.ds(t * 16 + 8, 8)
        send_b[rows, :] = jnp.where(lane1 < 64, send_b[rows, :], sums8)
    copies_b = []
    for k in range(1, 8):
        to = (z + k) % 8
        c = pltpu.make_async_remote_copy(
            src_ref=send_b.at[pl.ds(pl.multiple_of(to * 16, 16), 16)],
            dst_ref=recv_b.at[pl.ds(pl.multiple_of(z * 16, 16), 16)],
            send_sem=sb.at[k], recv_sem=rb.at[k],
            device_id=(row, to * 8 + g), device_id_type=MESH,
        )
        c.start()
        copies_b.append(c)
    mine = pl.ds(pl.multiple_of(z * 16, 16), 16)
    recv_b[mine, :] = send_b[mine, :]

    for i in range(8):
        slabs[i].wait()

        @pl.loop(0, 8)
        def _(q):
            v = sf[i, q]
            hi = v.astype(BF)
            at16 = pl.ds(pl.multiple_of((i % 2) * 128 + q * 16, 16), 16)
            sh[i // 2, at16, :] = hi
            sl[i // 2, at16, :] = (v - hi.astype(F32)).astype(BF)

    for c in copies_b:
        c.wait_recv()

    val = jnp.concatenate([recv_b[pl.ds(16 * s, 8), :] for s in range(8)], axis=0)
    loc = jnp.concatenate([recv_b[pl.ds(16 * s + 8, 8), :] for s in range(8)], axis=0)
    low32 = lax.broadcasted_iota(jnp.int32, (32, 128), 1) < 64
    pole_r = jnp.where(low32, val[:32], pltpu.roll(val[32:], 64, 1))
    coup_r = jnp.where(low32, pltpu.roll(val[:32], 64, 1), val[32:])
    loc_r = jnp.where(low32, loc[:32], pltpu.roll(loc[32:], 64, 1)).astype(jnp.int32)
    loc_h = loc_r >> 7
    loc_l = loc_r & 127
    parts = (*split3(pole_r), *split3(coup_r))
    id128 = lax.broadcasted_iota(jnp.int32, (128, 128), 0)
    id8 = lax.broadcasted_iota(jnp.int32, (8, 128), 0)
    for b in range(32):
        lanes = pl.ds(128 * b, 128)
        place_l[:, lanes] = (loc_l[b:b + 1, :] == id128).astype(F32).astype(BF)
        hit = loc_h[b:b + 1, :] == id8
        place_r[:, lanes] = jnp.concatenate(
            [jnp.where(hit, v[b:b + 1, :], 0.0) for v in parts], axis=0
        ).astype(BF)
    placed = dot_nt(place_r[...], place_l[...])
    pole_p = (placed[0:8] + placed[8:16]) + placed[16:24]
    coup_p = (placed[24:32] + placed[32:40]) + placed[40:48]
    for h in range(8):
        e = coup_p[h:h + 1, :] / (pole_p[h:h + 1, :] - roots_t)
        hi = e.astype(BF)
        lanes = pl.ds(128 * h, 128)
        entry[pl.ds(0, 128), lanes] = hi
        entry[pl.ds(128, 128), lanes] = (e - hi.astype(F32)).astype(BF)

    tot = jnp.sum(jnp.concatenate([recv_b[pl.ds(16 * s + 8, 8), :].reshape(1, 8, 128) for s in range(8)], axis=0), axis=0)
    tot_row = jnp.where(lane1[:1] < 64, pltpu.roll(tot, 64, 1)[0:1], tot[1:2])
    tot8 = jnp.broadcast_to(tot_row, (8, 128))

    copies_c = {}
    copies_x = {}

    def pass_x(o):
        copies_c[o].wait_recv()
        send_x[o] = prod[o, core] + recv_c[o]
        if o:
            to = (x + o) % 4
            c = pltpu.make_async_remote_copy(
                src_ref=send_x.at[o], dst_ref=recv_x.at[o], send_sem=sx.at[o], recv_sem=rx.at[o],
                device_id=(row, z * 8 + to * 2 + core), device_id_type=MESH,
            )
            c.start()
            copies_x[o] = c

    last = None
    for o in ORDER_X:
        xp = (x + o) % 4
        r1 = dot_nt(sh[xp], entry[...])
        r2 = dot_nt(sl[xp], entry[pl.ds(0, 128), :])
        p = (r1[:, 128:] + r2) + r1[:, :128]
        prod[o, :, pl.ds(0, 128), :] = p.reshape(2, 128, 128)
        prod[o, :, pl.ds(128, 8), :] = jnp.broadcast_to(tot8.reshape(1, 8, 128), (2, 8, 128))
        c = pltpu.make_async_remote_copy(
            src_ref=prod.at[o, 1 - core], dst_ref=recv_c.at[o], send_sem=sc.at[o], recv_sem=rc.at[o],
            device_id=(row, z * 8 + x * 2 + (1 - core)), device_id_type=MESH,
        )
        c.start()
        copies_c[o] = c
        if last is not None:
            pass_x(last)
        last = o
    pass_x(last)
    total = send_x[0]
    for o in (1, 3, 2):
        copies_x[o].wait_recv()
        total = total + recv_x[o]
    send_z[...] = total[:128].reshape(8, 16, 128)
    scale = lax.rsqrt(total[128:129])
    copies_z = []
    for k in range(1, 8):
        to = (z + k) % 8
        c = pltpu.make_async_remote_copy(
            src_ref=send_z.at[to], dst_ref=recv_z.at[k], send_sem=sz.at[k], recv_sem=rz.at[k],
            device_id=(row, to * 8 + g), device_id_type=MESH,
        )
        c.start()
        copies_z.append(c)
    final = send_z[z]
    for k, c in enumerate(copies_z):
        c.wait_recv()
        final = final + recv_z[k + 1]
    out_ref[...] = final * scale
    for c in copies_a + copies_b + list(copies_c.values()) + list(copies_x.values()) + copies_z:
        c.wait_send()


def body(eigen_slab, secular_poles, coupling, window_roots, deflated, column_map):
    hbm = pl.BlockSpec(memory_space=pl.ANY)
    dma = pltpu.SemaphoreType.DMA
    return pl.pallas_call(
        kernel,
        out_shape=jax.ShapeDtypeStruct((16, 128), F32),
        in_specs=[hbm] * 6,
        out_specs=pl.BlockSpec(memory_space=pltpu.VMEM),
        scratch_shapes=[
            pltpu.VMEM((8, 8, 16, 1024), F32),
            pltpu.VMEM((4, 256, 1024), BF),
            pltpu.VMEM((4, 256, 1024), BF),
            pltpu.VMEM((16, 128), F32),
            pltpu.VMEM((16, 128), F32),
            pltpu.VMEM((1, 128), F32),
            pltpu.VMEM((16, 128), jnp.int32),
            pltpu.VMEM((16, 128), jnp.int32),
            pltpu.VMEM((512, 2048), BF),
            pltpu.VMEM((1024, 128), BF),
            pltpu.VMEM((128, 2048), BF),
            pltpu.VMEM((8, 2, 8, 128), F32),
            pltpu.VMEM((8, 2, 8, 128), F32),
            pltpu.VMEM((128, 128), F32),
            pltpu.VMEM((128, 128), F32),
            pltpu.VMEM((128, 4096), BF),
            pltpu.VMEM((48, 4096), BF),
            pltpu.VMEM((256, 1024), BF),
            pltpu.VMEM((4, 2, 136, 128), F32),
            pltpu.VMEM((4, 136, 128), F32),
            pltpu.VMEM((4, 136, 128), F32),
            pltpu.VMEM((4, 136, 128), F32),
            pltpu.VMEM((8, 16, 128), F32),
            pltpu.VMEM((8, 16, 128), F32),
            dma((5,)), dma((8,)),
            dma((8,)), dma((8,)), dma((8,)), dma((8,)),
            dma((4,)), dma((4,)), dma((4,)), dma((4,)),
            dma((8,)), dma((8,)),
        ],
        compiler_params=pltpu.CompilerParams(
            collective_id=0, has_side_effects=True, vmem_limit_bytes=40 * 1024 * 1024
        ),
        name="top_merge",
    )(
        eigen_slab.reshape(8, 4, 2, 16, 1024),
        secular_poles.reshape(16, 128),
        coupling.reshape(16, 128),
        window_roots.reshape(1, 128),
        deflated.reshape(16, 128),
        column_map.reshape(16, 128),
    )


def solution(mesh):
    return jax.shard_map(
        body,
        mesh=mesh,
        in_specs=(P("row", "col"), P("col"), P("col"), P(), P("col"), P("col")),
        out_specs=P(("row", "col"), None),
        check_vma=False,
    )
```

```python
import jax
import jax.numpy as jnp
from jax import lax
from jax.experimental import pallas as pl
from jax.experimental.pallas import tpu as pltpu
from jax.sharding import PartitionSpec as P

MESH = pl.DeviceIdType.MESH
BF = jnp.bfloat16
F32 = jnp.float32
NT = (((1,), (1,)), ((), ()))
HALF = 65536
ORDER_X = (2, 1, 3, 0)


def dot_nt(a, b):
    return lax.dot_general(a, b, NT, preferred_element_type=F32)


def split3(v):
    hi = v.astype(BF)
    rest = v - hi.astype(F32)
    mid = rest.astype(BF)
    low = (rest - mid.astype(F32)).astype(BF)
    return hi.astype(F32), mid.astype(F32), low.astype(F32)


def kernel(
    slab, poles_in, coup_in, roots_in, defl_in, cmap_in, out_ref,
    sf, sh, sl, poles, coup, roots, defl, cmap,
    pieces, hots, slots, outgoing, recv_a, send_b, recv_b,
    place_l, place_r, entry, prod, recv_c, send_x, recv_x, send_z, recv_z,
    in_sem, slab_sem, sa, ra, sb, rb, sc, rc, sx, rx, sz, rz,
):
    row = lax.axis_index("row")
    col = lax.axis_index("col")
    z = col // 8
    g = col % 8
    x = g // 2
    core = g % 2

    barrier = pltpu.get_barrier_semaphore()
    for k in range(1, 8):
        pl.semaphore_signal(barrier, inc=1, device_id=(row, z * 8 + (g + k) % 8), device_id_type=MESH)
        pl.semaphore_signal(barrier, inc=1, device_id=(row, ((z + k) % 8) * 8 + g), device_id_type=MESH)

    smalls = [
        pltpu.make_async_copy(s, d, in_sem.at[i])
        for i, (s, d) in enumerate(
            [(cmap_in, cmap), (poles_in, poles), (coup_in, coup), (defl_in, defl), (roots_in, roots)]
        )
    ]
    for c in smalls:
        c.start()
    slabs = [
        pltpu.make_async_copy(slab.at[:, i // 2, i % 2], sf.at[i], slab_sem.at[i]) for i in range(8)
    ]
    for c in slabs:
        c.start()

    for c in smalls:
        c.wait()

    cm = cmap[...]
    upper = (cm >= HALF).astype(jnp.int32)
    within = cm - upper * HALF
    target = within >> 10
    local = within & 1023
    order = (target & 7) * 8 + (target >> 3)
    order = jnp.where(upper == row // 4, order, -1)
    pole_v = poles[...]
    coup_v = jnp.where(defl[...] == 0, coup[...], 0.0)
    coup[...] = coup_v
    vals = (
        *split3(pole_v),
        *split3(coup_v),
        (local >> 7).astype(F32),
        (local & 127).astype(F32),
    )
    dest_id = lax.broadcasted_iota(jnp.int32, (64, 128), 0)
    slot_id = (lax.broadcasted_iota(jnp.int32, (128, 128), 0) & 63).astype(F32)
    for b in range(16):
        hots[pl.ds(64 * b, 64), :] = (order[b:b + 1, :] == dest_id).astype(F32).astype(BF)
    before = lax.broadcasted_iota(jnp.int32, (128, 256), 0)
    at = lax.broadcasted_iota(jnp.int32, (128, 256), 1)
    tri = ((before < at) | (at >= 128)).astype(F32).astype(BF)
    counts = jnp.dot(hots[...], tri, preferred_element_type=F32)
    carry = jnp.zeros((64, 128), F32)
    for b in range(16):
        lanes = pl.ds(128 * b, 128)
        hot = hots[pl.ds(64 * b, 64), :]
        block = counts[64 * b:64 * b + 64]
        rank = jnp.sum(hot.astype(F32) * (block[:, :128] + carry), axis=0, keepdims=True)
        carry = carry + block[:, 128:]
        slots[:, lanes] = (rank == slot_id).astype(F32).astype(BF)
        for i, v in enumerate(vals):
            pieces[pl.ds(64 * i, 64), lanes] = hot * jnp.broadcast_to(v[b:b + 1, :], (64, 128)).astype(BF)
    routed = dot_nt(pieces[...], slots[...])
    pole_o = (routed[0:64] + routed[64:128]) + routed[128:192]
    coup_o = (routed[192:256] + routed[256:320]) + routed[320:384]
    at_o = routed[384:448] * 128.0 + routed[448:512]
    low_lane = lax.broadcasted_iota(jnp.int32, (64, 128), 1) < 64
    outgoing[:, 0] = jnp.where(low_lane, pole_o, coup_o).reshape(8, 8, 128)
    outgoing[:, 1] = at_o.reshape(8, 8, 128)

    pl.semaphore_wait(barrier, 14)
    copies_a = []
    for k in range(1, 8):
        to = (g + k) % 8
        c = pltpu.make_async_remote_copy(
            src_ref=outgoing.at[to], dst_ref=recv_a.at[g], send_sem=sa.at[k], recv_sem=ra.at[k],
            device_id=(row, z * 8 + to), device_id_type=MESH,
        )
        c.start()
        copies_a.append(c)
    recv_a[g] = outgoing[g]

    roots_t = jnp.transpose(jnp.broadcast_to(roots[...], (128, 128)))
    sums = jnp.zeros((128, 128), F32)
    for b in range(16):
        e = coup_v[b:b + 1, :] / (pole_v[b:b + 1, :] - roots_t)
        sums = sums + e * e
    sums = jnp.sum(jnp.transpose(sums), axis=0, keepdims=True)
    lane1 = lax.broadcasted_iota(jnp.int32, (8, 128), 1)
    sub1 = lax.broadcasted_iota(jnp.int32, (8, 128), 0)
    sums8 = jnp.broadcast_to(sums, (8, 128))
    sums8 = jnp.where(sub1 == 0, pltpu.roll(sums8, 64, 1), sums8)

    for c in copies_a:
        c.wait_recv()
    for s in range(8):
        for k in range(2):
            send_b[pl.ds(k * 8 + s, 8, stride=16), :] = recv_a[s, k]
    for t in range(8):
        rows = pl.ds(t * 16 + 8, 8)
        send_b[rows, :] = jnp.where(lane1 < 64, send_b[rows, :], sums8)
    copies_b = []
    for k in range(1, 8):
        to = (z + k) % 8
        c = pltpu.make_async_remote_copy(
            src_ref=send_b.at[pl.ds(pl.multiple_of(to * 16, 16), 16)],
            dst_ref=recv_b.at[pl.ds(pl.multiple_of(z * 16, 16), 16)],
            send_sem=sb.at[k], recv_sem=rb.at[k],
            device_id=(row, to * 8 + g), device_id_type=MESH,
        )
        c.start()
        copies_b.append(c)
    mine = pl.ds(pl.multiple_of(z * 16, 16), 16)
    recv_b[mine, :] = send_b[mine, :]

    for i in range(8):
        slabs[i].wait()

        @pl.loop(0, 8)
        def _(q):
            v = sf[i, q]
            hi = v.astype(BF)
            at16 = pl.ds(pl.multiple_of((i % 2) * 128 + q * 16, 16), 16)
            sh[i // 2, at16, :] = hi
            sl[i // 2, at16, :] = (v - hi.astype(F32)).astype(BF)

    for c in copies_b:
        c.wait_recv()

    val = jnp.concatenate([recv_b[pl.ds(16 * s, 8), :] for s in range(8)], axis=0)
    loc = jnp.concatenate([recv_b[pl.ds(16 * s + 8, 8), :] for s in range(8)], axis=0)
    low32 = lax.broadcasted_iota(jnp.int32, (32, 128), 1) < 64
    pole_r = jnp.where(low32, val[:32], pltpu.roll(val[32:], 64, 1))
    coup_r = jnp.where(low32, pltpu.roll(val[:32], 64, 1), val[32:])
    loc_r = jnp.where(low32, loc[:32], pltpu.roll(loc[32:], 64, 1)).astype(jnp.int32)
    loc_h = loc_r >> 7
    loc_l = loc_r & 127
    parts = (*split3(pole_r), *split3(coup_r))
    id128 = lax.broadcasted_iota(jnp.int32, (128, 128), 0)
    id8 = lax.broadcasted_iota(jnp.int32, (8, 128), 0)
    for b in range(32):
        lanes = pl.ds(128 * b, 128)
        place_l[:, lanes] = (loc_l[b:b + 1, :] == id128).astype(F32).astype(BF)
        hit = loc_h[b:b + 1, :] == id8
        place_r[:, lanes] = jnp.concatenate(
            [jnp.where(hit, v[b:b + 1, :], 0.0) for v in parts], axis=0
        ).astype(BF)
    placed = dot_nt(place_r[...], place_l[...])
    pole_p = (placed[0:8] + placed[8:16]) + placed[16:24]
    coup_p = (placed[24:32] + placed[32:40]) + placed[40:48]
    for h in range(8):
        e = coup_p[h:h + 1, :] / (pole_p[h:h + 1, :] - roots_t)
        hi = e.astype(BF)
        lanes = pl.ds(128 * h, 128)
        entry[pl.ds(0, 128), lanes] = hi
        entry[pl.ds(128, 128), lanes] = (e - hi.astype(F32)).astype(BF)

    tot = jnp.sum(jnp.concatenate([recv_b[pl.ds(16 * s + 8, 8), :].reshape(1, 8, 128) for s in range(8)], axis=0), axis=0)
    tot_row = jnp.where(lane1[:1] < 64, pltpu.roll(tot, 64, 1)[0:1], tot[1:2])
    tot8 = jnp.broadcast_to(tot_row, (8, 128))

    copies_c = {}
    copies_x = {}

    def pass_x(o):
        copies_c[o].wait_recv()
        send_x[o] = prod[o, core] + recv_c[o]
        if o:
            to = (x + o) % 4
            c = pltpu.make_async_remote_copy(
                src_ref=send_x.at[o], dst_ref=recv_x.at[o], send_sem=sx.at[o], recv_sem=rx.at[o],
                device_id=(row, z * 8 + to * 2 + core), device_id_type=MESH,
            )
            c.start()
            copies_x[o] = c

    last = None
    for o in ORDER_X:
        xp = (x + o) % 4
        r1 = dot_nt(sh[xp], entry[...])
        r2 = dot_nt(sl[xp], entry[pl.ds(0, 128), :])
        p = (r1[:, 128:] + r2) + r1[:, :128]
        prod[o, :, pl.ds(0, 128), :] = p.reshape(2, 128, 128)
        prod[o, :, pl.ds(128, 8), :] = jnp.broadcast_to(tot8.reshape(1, 8, 128), (2, 8, 128))
        c = pltpu.make_async_remote_copy(
            src_ref=prod.at[o, 1 - core], dst_ref=recv_c.at[o], send_sem=sc.at[o], recv_sem=rc.at[o],
            device_id=(row, z * 8 + x * 2 + (1 - core)), device_id_type=MESH,
        )
        c.start()
        copies_c[o] = c
        if last is not None:
            pass_x(last)
        last = o
    pass_x(last)
    total = send_x[0]
    for o in (1, 3, 2):
        copies_x[o].wait_recv()
        total = total + recv_x[o]
    send_z[...] = total[:128].reshape(8, 16, 128)
    scale = lax.rsqrt(total[128:129])
    copies_z = []
    for k in range(1, 8):
        to = (z + k) % 8
        c = pltpu.make_async_remote_copy(
            src_ref=send_z.at[to], dst_ref=recv_z.at[k], send_sem=sz.at[k], recv_sem=rz.at[k],
            device_id=(row, to * 8 + g), device_id_type=MESH,
        )
        c.start()
        copies_z.append(c)
    final = send_z[z]
    for k, c in enumerate(copies_z):
        c.wait_recv()
        final = final + recv_z[k + 1]
    out_ref[...] = final * scale
    for c in copies_a + copies_b + list(copies_c.values()) + list(copies_x.values()) + copies_z:
        c.wait_send()


def body(eigen_slab, secular_poles, coupling, window_roots, deflated, column_map):
    hbm = pl.BlockSpec(memory_space=pltpu.HBM)
    dma = pltpu.SemaphoreType.DMA
    return pl.pallas_call(
        kernel,
        out_shape=jax.ShapeDtypeStruct((16, 128), F32),
        in_specs=[hbm] * 6,
        out_specs=pl.BlockSpec(memory_space=pltpu.VMEM),
        scratch_shapes=[
            pltpu.VMEM((8, 8, 16, 1024), F32),
            pltpu.VMEM((4, 256, 1024), BF),
            pltpu.VMEM((4, 256, 1024), BF),
            pltpu.VMEM((16, 128), F32),
            pltpu.VMEM((16, 128), F32),
            pltpu.VMEM((1, 128), F32),
            pltpu.VMEM((16, 128), jnp.int32),
            pltpu.VMEM((16, 128), jnp.int32),
            pltpu.VMEM((512, 2048), BF),
            pltpu.VMEM((1024, 128), BF),
            pltpu.VMEM((128, 2048), BF),
            pltpu.VMEM((8, 2, 8, 128), F32),
            pltpu.VMEM((8, 2, 8, 128), F32),
            pltpu.VMEM((128, 128), F32),
            pltpu.VMEM((128, 128), F32),
            pltpu.VMEM((128, 4096), BF),
            pltpu.VMEM((48, 4096), BF),
            pltpu.VMEM((256, 1024), BF),
            pltpu.VMEM((4, 2, 136, 128), F32),
            pltpu.VMEM((4, 136, 128), F32),
            pltpu.VMEM((4, 136, 128), F32),
            pltpu.VMEM((4, 136, 128), F32),
            pltpu.VMEM((8, 16, 128), F32),
            pltpu.VMEM((8, 16, 128), F32),
            dma((5,)), dma((8,)),
            dma((8,)), dma((8,)), dma((8,)), dma((8,)),
            dma((4,)), dma((4,)), dma((4,)), dma((4,)),
            dma((8,)), dma((8,)),
        ],
        compiler_params=pltpu.CompilerParams(
            collective_id=0, has_side_effects=True, vmem_limit_bytes=40 * 1024 * 1024
        ),
        name="top_merge",
    )(
        *(
            pltpu.with_memory_space_constraint(v, pltpu.HBM)
            for v in (
                eigen_slab.reshape(8, 4, 2, 16, 1024),
                secular_poles.reshape(16, 128),
                coupling.reshape(16, 128),
                window_roots.reshape(1, 128),
                deflated.reshape(16, 128),
                column_map.reshape(16, 128),
            )
        )
    )


def solution(mesh):
    return jax.shard_map(
        body,
        mesh=mesh,
        in_specs=(P("row", "col"), P("col"), P("col"), P(), P("col"), P("col")),
        out_specs=P(("row", "col"), None),
        check_vma=False,
    )
```

```python
import jax
import jax.numpy as jnp
from jax import lax
from jax.experimental import pallas as pl
from jax.experimental.pallas import tpu as pltpu
from jax.sharding import PartitionSpec as P

MESH = pl.DeviceIdType.MESH
BF = jnp.bfloat16
F32 = jnp.float32
NT = (((1,), (1,)), ((), ()))
HALF = 65536
STEPS_Z = (4, 3, 5, 2, 6, 1, 7, 0)
STEPS_X = (2, 1, 3, 0)


def dot_nt(a, b):
    return lax.dot_general(a, b, NT, preferred_element_type=F32)


def split3(v):
    hi = v.astype(BF)
    rest = v - hi.astype(F32)
    mid = rest.astype(BF)
    low = (rest - mid.astype(F32)).astype(BF)
    return hi.astype(F32), mid.astype(F32), low.astype(F32)


def kernel(
    slab, poles_in, coup_in, roots_in, defl_in, cmap_in, out_ref,
    sf, sh, sl, poles, coup, roots, defl, cmap,
    pieces, hots, slots, outgoing, recv_a, recv_b, pass_b,
    place_l, place_r, entry, prod, recv_c, send_r, recv_r,
    in_sem, slab_sem, sa, ra, sb, rb, sc, rc, sr, rr,
):
    row = lax.axis_index("row")
    col = lax.axis_index("col")
    chip = col // 2
    z = chip // 4
    x = chip % 4
    core = col % 2
    sibling = (row, chip * 2 + (1 - core))
    others = [
        ((z + dz) % 8 * 4 + (x + dx) % 4) for dz in STEPS_Z for dx in STEPS_X if dz or dx
    ]

    barrier = pltpu.get_barrier_semaphore()
    for to in others:
        pl.semaphore_signal(barrier, inc=1, device_id=(row, to * 2 + core), device_id_type=MESH)
    pl.semaphore_signal(barrier, inc=1, device_id=sibling, device_id_type=MESH)

    smalls = [
        pltpu.make_async_copy(s, d, in_sem.at[i])
        for i, (s, d) in enumerate(
            [(cmap_in, cmap), (poles_in, poles), (coup_in, coup), (defl_in, defl), (roots_in, roots)]
        )
    ]
    for c in smalls:
        c.start()
    slabs = [
        pltpu.make_async_copy(slab.at[pl.ds(i // 2 * 2, 2), :, i % 2], sf.at[i], slab_sem.at[i]) for i in range(8)
    ]
    for c in slabs:
        c.start()

    for c in smalls:
        c.wait()

    cm = cmap[...]
    upper = (cm >= HALF).astype(jnp.int32)
    within = cm - upper * HALF
    target = within >> 10
    local = within & 1023
    order = (target & 1) * 32 + (target >> 1)
    order = jnp.where(upper == row // 4, order, -1)
    pole_v = poles[...]
    coup_v = jnp.where(defl[...] == 0, coup[...], 0.0)
    vals = (
        *split3(pole_v),
        *split3(coup_v),
        (local >> 7).astype(F32),
        (local & 127).astype(F32),
    )
    dest_id = lax.broadcasted_iota(jnp.int32, (64, 128), 0)
    slot_id = (lax.broadcasted_iota(jnp.int32, (128, 128), 0) & 63).astype(F32)
    for b in range(16):
        hots[pl.ds(64 * b, 64), :] = (order[b:b + 1, :] == dest_id).astype(F32).astype(BF)
    before = lax.broadcasted_iota(jnp.int32, (128, 256), 0)
    at = lax.broadcasted_iota(jnp.int32, (128, 256), 1)
    tri = ((before < at) | (at >= 128)).astype(F32).astype(BF)
    counts = jnp.dot(hots[...], tri, preferred_element_type=F32)
    carry = jnp.zeros((64, 128), F32)
    for b in range(16):
        lanes = pl.ds(128 * b, 128)
        hot = hots[pl.ds(64 * b, 64), :]
        block = counts[64 * b:64 * b + 64]
        rank = jnp.sum(hot.astype(F32) * (block[:, :128] + carry), axis=0, keepdims=True)
        carry = carry + block[:, 128:]
        slots[:, lanes] = (rank == slot_id).astype(F32).astype(BF)
        for i, v in enumerate(vals):
            pieces[pl.ds(64 * i, 64), lanes] = hot * jnp.broadcast_to(v[b:b + 1, :], (64, 128)).astype(BF)
    routed = dot_nt(pieces[...], slots[...])
    pole_o = (routed[0:64] + routed[64:128]) + routed[128:192]
    coup_o = (routed[192:256] + routed[256:320]) + routed[320:384]
    at_o = routed[384:448] * 128.0 + routed[448:512]
    roots_t = jnp.transpose(jnp.broadcast_to(roots[...], (128, 128)))
    sums = jnp.zeros((128, 128), F32)
    for b in range(16):
        e = coup_v[b:b + 1, :] / (pole_v[b:b + 1, :] - roots_t)
        sums = sums + e * e
    sums = jnp.sum(jnp.transpose(sums), axis=0, keepdims=True)
    low_lane = lax.broadcasted_iota(jnp.int32, (32, 128), 1) < 64
    for i, v in enumerate((pole_o, coup_o, at_o)):
        outgoing[i] = jnp.where(low_lane, v[:32], v[32:])
    outgoing[3] = jnp.broadcast_to(sums, (32, 128))

    pl.semaphore_wait(barrier, 32)
    copies_a = []
    for k, to in enumerate(others):
        c = pltpu.make_async_remote_copy(
            src_ref=outgoing.at[:, pl.ds(to, 1)], dst_ref=recv_a.at[:, pl.ds(chip, 1)],
            send_sem=sa.at[k], recv_sem=ra.at[k],
            device_id=(row, to * 2 + core), device_id_type=MESH,
        )
        c.start()
        copies_a.append(c)

    for i in range(8):
        slabs[i].wait()

        @pl.loop(0, 8)
        def _(q):
            v = sf[i, q // 4, q % 4]
            hi = v.astype(BF)
            at16 = pl.ds(pl.multiple_of((i % 2) * 128 + q * 16, 16), 16)
            sh[i // 2, at16, :] = hi
            sl[i // 2, at16, :] = (v - hi.astype(F32)).astype(BF)

    for c in copies_a:
        c.wait_recv()
    here = lax.broadcasted_iota(jnp.int32, (32, 128), 0) == chip
    for i in range(4):
        v = jnp.where(here, outgoing[i], recv_a[i])
        pass_b[i] = v if i < 3 else jnp.broadcast_to(jnp.sum(v, axis=0, keepdims=True), (32, 128))
    pair = pltpu.make_async_remote_copy(
        src_ref=pass_b, dst_ref=recv_b, send_sem=sb.at[0], recv_sem=rb.at[0],
        device_id=sibling, device_id_type=MESH,
    )
    pair.start()
    pair.wait_recv()

    own_lane = (lax.broadcasted_iota(jnp.int32, (32, 128), 1) >> 6) == core
    pole_r, coup_r, loc_r = (
        jnp.where(own_lane, pass_b[i], pltpu.roll(recv_b[i], 64, 1)) for i in range(3)
    )
    scale = lax.rsqrt(pass_b[3, 0:1, :] + recv_b[3, 0:1, :])
    loc_r = loc_r.astype(jnp.int32)
    loc_h = loc_r >> 7
    loc_l = loc_r & 127
    parts = (*split3(pole_r), *split3(coup_r))
    id128 = lax.broadcasted_iota(jnp.int32, (128, 128), 0)
    id8 = lax.broadcasted_iota(jnp.int32, (8, 128), 0)
    for b in range(32):
        lanes = pl.ds(128 * b, 128)
        place_l[:, lanes] = (loc_l[b:b + 1, :] == id128).astype(F32).astype(BF)
        hit = loc_h[b:b + 1, :] == id8
        place_r[:, lanes] = jnp.concatenate(
            [jnp.where(hit, v[b:b + 1, :], 0.0) for v in parts], axis=0
        ).astype(BF)
    placed = dot_nt(place_r[...], place_l[...])
    pole_p = (placed[0:8] + placed[8:16]) + placed[16:24]
    coup_p = (placed[24:32] + placed[32:40]) + placed[40:48]
    for h in range(8):
        e = coup_p[h:h + 1, :] / (pole_p[h:h + 1, :] - roots_t)
        hi = e.astype(BF)
        lanes = pl.ds(128 * h, 128)
        entry[pl.ds(0, 128), lanes] = hi
        entry[pl.ds(128, 128), lanes] = (e - hi.astype(F32)).astype(BF)

    copies_c = []
    copies_r = []

    def send_on(m):
        copies_c[m].wait_recv()
        send_r[pl.ds(8 * m, 8)] = (prod[m, core] + recv_c[m]).reshape(8, 16, 128)
        for i in range(8):
            to = (2 * m + i // 4) * 4 + (x + STEPS_X[i % 4]) % 4

            @pl.when(to != chip)
            def _():
                remote(to).start()

    def remote(to):
        return pltpu.make_async_remote_copy(
            src_ref=send_r.at[to], dst_ref=recv_r.at[chip], send_sem=sr.at[to], recv_sem=rr.at[chip],
            device_id=(row, to * 2 + core), device_id_type=MESH,
        )

    for m in range(4):
        r1 = dot_nt(sh[m], entry[...])
        r2 = dot_nt(sl[m], entry[pl.ds(0, 128), :])
        p = (r1[:, 128:] + r2) + r1[:, :128]
        prod[m] = p.reshape(2, 128, 128)
        c = pltpu.make_async_remote_copy(
            src_ref=prod.at[m, 1 - core], dst_ref=recv_c.at[m], send_sem=sc.at[m], recv_sem=rc.at[m],
            device_id=sibling, device_id_type=MESH,
        )
        c.start()
        copies_c.append(c)
        if m:
            send_on(m - 1)
    send_on(3)
    final = send_r[chip]
    for to in others:
        pltpu.make_async_remote_copy(
            src_ref=send_r.at[to], dst_ref=recv_r.at[to], send_sem=sr.at[to], recv_sem=rr.at[to],
            device_id=(row, to * 2 + core), device_id_type=MESH,
        ).wait_recv()
        final = final + recv_r[to]
    out_ref[...] = final * scale
    for to in others:
        remote(to).wait_send()
    for c in [*copies_a, pair, *copies_c]:
        c.wait_send()


def body(eigen_slab, secular_poles, coupling, window_roots, deflated, column_map):
    hbm = pl.BlockSpec(memory_space=pltpu.HBM)
    dma = pltpu.SemaphoreType.DMA
    return pl.pallas_call(
        kernel,
        out_shape=jax.ShapeDtypeStruct((16, 128), F32),
        in_specs=[hbm] * 6,
        out_specs=pl.BlockSpec(memory_space=pltpu.VMEM),
        scratch_shapes=[
            pltpu.VMEM((8, 2, 4, 16, 1024), F32),
            pltpu.VMEM((4, 256, 1024), BF),
            pltpu.VMEM((4, 256, 1024), BF),
            pltpu.VMEM((16, 128), F32),
            pltpu.VMEM((16, 128), F32),
            pltpu.VMEM((1, 128), F32),
            pltpu.VMEM((16, 128), jnp.int32),
            pltpu.VMEM((16, 128), jnp.int32),
            pltpu.VMEM((512, 2048), BF),
            pltpu.VMEM((1024, 128), BF),
            pltpu.VMEM((128, 2048), BF),
            pltpu.VMEM((4, 32, 128), F32),
            pltpu.VMEM((4, 32, 128), F32),
            pltpu.VMEM((4, 32, 128), F32),
            pltpu.VMEM((4, 32, 128), F32),
            pltpu.VMEM((128, 4096), BF),
            pltpu.VMEM((48, 4096), BF),
            pltpu.VMEM((256, 1024), BF),
            pltpu.VMEM((4, 2, 128, 128), F32),
            pltpu.VMEM((4, 128, 128), F32),
            pltpu.VMEM((32, 16, 128), F32),
            pltpu.VMEM((32, 16, 128), F32),
            dma((5,)), dma((8,)),
            dma((31,)), dma((31,)), dma((1,)), dma((1,)),
            dma((4,)), dma((4,)), dma((32,)), dma((32,)),
        ],
        compiler_params=pltpu.CompilerParams(
            collective_id=0, has_side_effects=True, vmem_limit_bytes=40 * 1024 * 1024
        ),
        name="top_merge",
    )(
        *(
            pltpu.with_memory_space_constraint(v, pltpu.HBM)
            for v in (
                eigen_slab.reshape(8, 4, 2, 16, 1024),
                secular_poles.reshape(16, 128),
                coupling.reshape(16, 128),
                window_roots.reshape(1, 128),
                deflated.reshape(16, 128),
                column_map.reshape(16, 128),
            )
        )
    )


def solution(mesh):
    return jax.shard_map(
        body,
        mesh=mesh,
        in_specs=(P("row", "col"), P("col"), P("col"), P(), P("col"), P("col")),
        out_specs=P(("row", "col"), None),
        check_vma=False,
    )
```

```python
import jax
import jax.numpy as jnp
from jax import lax
from jax.experimental import pallas as pl
from jax.experimental.pallas import tpu as pltpu
from jax.sharding import PartitionSpec as P

MESH = pl.DeviceIdType.MESH
BF = jnp.bfloat16
F32 = jnp.float32
NT = (((1,), (1,)), ((), ()))
HALF = 65536
STEPS_Z = (4, 3, 5, 2, 6, 1, 7, 0)
STEPS_X = (2, 1, 3, 0)


def dot_nt(a, b):
    return lax.dot_general(a, b, NT, preferred_element_type=F32)


def split3(v):
    hi = v.astype(BF)
    rest = v - hi.astype(F32)
    mid = rest.astype(BF)
    low = (rest - mid.astype(F32)).astype(BF)
    return hi.astype(F32), mid.astype(F32), low.astype(F32)


def kernel(
    slab, poles_in, coup_in, roots_in, defl_in, cmap_in, out_ref,
    sf, sh, sl, poles, coup, roots, defl, cmap,
    pieces, hots, slots, outgoing, recv_a, recv_b, pass_b,
    place_l, place_r, entry, prod, recv_c, send_r, recv_r,
    in_sem, slab_sem, sa, ra, sb, rb, sc, rc, sr, rr,
):
    row = lax.axis_index("row")
    col = lax.axis_index("col")
    chip = col // 2
    z = chip // 4
    x = chip % 4
    core = col % 2
    sibling = (row, chip * 2 + (1 - core))
    others = [
        lax.rem(z + dz, 8) * 4 + lax.rem(x + dx, 4) for dz in STEPS_Z for dx in STEPS_X if dz or dx
    ]

    smalls = [
        pltpu.make_async_copy(s, d, in_sem.at[i])
        for i, (s, d) in enumerate(
            [(cmap_in, cmap), (poles_in, poles), (coup_in, coup), (defl_in, defl), (roots_in, roots)]
        )
    ]
    for c in smalls:
        c.start()
    barrier = pltpu.get_barrier_semaphore()
    for to in others:
        pl.semaphore_signal(barrier, inc=1, device_id=(row, to * 2 + core), device_id_type=MESH)
    pl.semaphore_signal(barrier, inc=1, device_id=sibling, device_id_type=MESH)

    slabs = [
        pltpu.make_async_copy(slab.at[pl.ds(2 * i, 2)], sf.at[i], slab_sem.at[i]) for i in range(4)
    ]
    for c in slabs:
        c.start()

    for c in smalls:
        c.wait()

    cm = cmap[...]
    upper = (cm >= HALF).astype(jnp.int32)
    within = cm - upper * HALF
    target = within >> 10
    local = within & 1023
    order = (target & 1) * 32 + (target >> 1)
    order = jnp.where(upper == row // 4, order, -1)
    pole_v = poles[...]
    coup_v = jnp.where(defl[...] == 0, coup[...], 0.0)
    vals = (
        *split3(pole_v),
        *split3(coup_v),
        (local >> 7).astype(F32),
        (local & 127).astype(F32),
    )
    dest_id = lax.broadcasted_iota(jnp.int32, (64, 128), 0)
    slot_id = (lax.broadcasted_iota(jnp.int32, (128, 128), 0) & 63).astype(F32)
    for b in range(16):
        hots[pl.ds(64 * b, 64), :] = (order[b:b + 1, :] == dest_id).astype(F32).astype(BF)
    before = lax.broadcasted_iota(jnp.int32, (128, 256), 0)
    at = lax.broadcasted_iota(jnp.int32, (128, 256), 1)
    tri = ((before < at) | (at >= 128)).astype(F32).astype(BF)
    counts = jnp.dot(hots[...], tri, preferred_element_type=F32)
    carry = jnp.zeros((64, 128), F32)
    for b in range(16):
        lanes = pl.ds(128 * b, 128)
        hot = hots[pl.ds(64 * b, 64), :]
        block = counts[64 * b:64 * b + 64]
        rank = jnp.sum(hot.astype(F32) * (block[:, :128] + carry), axis=0, keepdims=True)
        carry = carry + block[:, 128:]
        slots[:, lanes] = (rank == slot_id).astype(F32).astype(BF)
        for i, v in enumerate(vals):
            pieces[pl.ds(64 * i, 64), lanes] = hot * jnp.broadcast_to(v[b:b + 1, :], (64, 128)).astype(BF)
    routed = dot_nt(pieces[...], slots[...])
    pole_o = (routed[0:64] + routed[64:128]) + routed[128:192]
    coup_o = (routed[192:256] + routed[256:320]) + routed[320:384]
    at_o = routed[384:448] * 128.0 + routed[448:512]
    roots_t = jnp.transpose(jnp.broadcast_to(roots[...], (128, 128)))
    sums = jnp.zeros((128, 128), F32)
    for b in range(16):
        e = coup_v[b:b + 1, :] / (pole_v[b:b + 1, :] - roots_t)
        sums = sums + e * e
    sums = jnp.sum(jnp.transpose(sums), axis=0, keepdims=True)
    low_lane = lax.broadcasted_iota(jnp.int32, (32, 128), 1) < 64
    for i, v in enumerate((pole_o, coup_o, at_o)):
        outgoing[i] = jnp.where(low_lane, v[:32], v[32:])
    outgoing[3] = jnp.broadcast_to(sums, (32, 128))

    pl.semaphore_wait(barrier, 32)
    for to in others:
        c = pltpu.make_async_remote_copy(
            src_ref=outgoing.at[:, pl.ds(to, 1)], dst_ref=recv_a.at[:, pl.ds(chip, 1)],
            send_sem=sa, recv_sem=ra,
            device_id=(row, to * 2 + core), device_id_type=MESH,
        )
        c.start()

    for m in range(4):
        slabs[m].wait()
        for half in range(2):

            @pl.loop(0, 8)
            def _(q):
                v = sf[m, q // 4, q % 4, half]
                hi = v.astype(BF)
                at16 = pl.ds(pl.multiple_of(half * 128 + q * 16, 16), 16)
                sh[m, at16, :] = hi
                sl[m, at16, :] = (v - hi.astype(F32)).astype(BF)

    all_a = pltpu.make_async_remote_copy(
        src_ref=outgoing.at[:, pl.ds(0, 31)], dst_ref=recv_a.at[:, pl.ds(0, 31)],
        send_sem=sa, recv_sem=ra, device_id=sibling, device_id_type=MESH,
    )
    all_a.wait_recv()
    here = lax.broadcasted_iota(jnp.int32, (32, 128), 0) == chip
    for i in range(4):
        v = jnp.where(here, outgoing[i], recv_a[i])
        pass_b[i] = v if i < 3 else jnp.broadcast_to(jnp.sum(v, axis=0, keepdims=True), (32, 128))
    pair = pltpu.make_async_remote_copy(
        src_ref=pass_b, dst_ref=recv_b, send_sem=sb, recv_sem=rb,
        device_id=sibling, device_id_type=MESH,
    )
    pair.start()
    pair.wait_recv()

    own_lane = (lax.broadcasted_iota(jnp.int32, (32, 128), 1) >> 6) == core
    pole_r, coup_r, loc_r = (
        jnp.where(own_lane, pass_b[i], pltpu.roll(recv_b[i], 64, 1)) for i in range(3)
    )
    scale = lax.rsqrt(pass_b[3, 0:1, :] + recv_b[3, 0:1, :])
    loc_r = loc_r.astype(jnp.int32)
    loc_h = loc_r >> 7
    loc_l = loc_r & 127
    parts = (*split3(pole_r), *split3(coup_r))
    id128 = lax.broadcasted_iota(jnp.int32, (128, 128), 0)
    id8 = lax.broadcasted_iota(jnp.int32, (8, 128), 0)
    for b in range(32):
        lanes = pl.ds(128 * b, 128)
        place_l[:, lanes] = (loc_l[b:b + 1, :] == id128).astype(F32).astype(BF)
        hit = loc_h[b:b + 1, :] == id8
        place_r[:, lanes] = jnp.concatenate(
            [jnp.where(hit, v[b:b + 1, :], 0.0) for v in parts], axis=0
        ).astype(BF)
    placed = dot_nt(place_r[...], place_l[...])
    pole_p = (placed[0:8] + placed[8:16]) + placed[16:24]
    coup_p = (placed[24:32] + placed[32:40]) + placed[40:48]
    for h in range(8):
        e = coup_p[h:h + 1, :] / (pole_p[h:h + 1, :] - roots_t)
        hi = e.astype(BF)
        lanes = pl.ds(128 * h, 128)
        entry[pl.ds(0, 128), lanes] = hi
        entry[pl.ds(128, 128), lanes] = (e - hi.astype(F32)).astype(BF)

    copies_c = []
    copies_r = []

    def send_on(m):
        copies_c[m].wait_recv()
        send_r[pl.ds(8 * m, 8)] = (prod[m, core] + recv_c[m]).reshape(8, 16, 128)
        for i in range(8):
            to = (2 * m + i // 4) * 4 + lax.rem(x + STEPS_X[i % 4], 4)

            @pl.when(to != chip)
            def _():
                remote(to).start()

    def remote(to):
        return pltpu.make_async_remote_copy(
            src_ref=send_r.at[to], dst_ref=recv_r.at[chip], send_sem=sr, recv_sem=rr,
            device_id=(row, to * 2 + core), device_id_type=MESH,
        )

    for m in range(4):
        r1 = dot_nt(sh[m], entry[...])
        r2 = dot_nt(sl[m], entry[pl.ds(0, 128), :])
        p = (r1[:, 128:] + r2) + r1[:, :128]
        prod[m] = p.reshape(2, 128, 128)
        c = pltpu.make_async_remote_copy(
            src_ref=prod.at[m, 1 - core], dst_ref=recv_c.at[m], send_sem=sc.at[m], recv_sem=rc.at[m],
            device_id=sibling, device_id_type=MESH,
        )
        c.start()
        copies_c.append(c)
        if m:
            send_on(m - 1)
    send_on(3)
    all_r = pltpu.make_async_remote_copy(
        src_ref=send_r.at[pl.ds(0, 31)], dst_ref=recv_r.at[pl.ds(0, 31)],
        send_sem=sr, recv_sem=rr, device_id=sibling, device_id_type=MESH,
    )
    all_r.wait_recv()
    final = send_r[chip]
    for to in others:
        final = final + recv_r[to]
    out_ref[...] = final * scale
    for c in [all_a, all_r, pair, *copies_c]:
        c.wait_send()


def body(eigen_slab, secular_poles, coupling, window_roots, deflated, column_map):
    hbm = pl.BlockSpec(memory_space=pltpu.HBM)
    dma = pltpu.SemaphoreType.DMA
    return pl.pallas_call(
        kernel,
        out_shape=jax.ShapeDtypeStruct((16, 128), F32),
        in_specs=[hbm] * 6,
        out_specs=pl.BlockSpec(memory_space=pltpu.VMEM),
        scratch_shapes=[
            pltpu.VMEM((4, 2, 4, 2, 16, 1024), F32),
            pltpu.VMEM((4, 256, 1024), BF),
            pltpu.VMEM((4, 256, 1024), BF),
            pltpu.VMEM((16, 128), F32),
            pltpu.VMEM((16, 128), F32),
            pltpu.VMEM((1, 128), F32),
            pltpu.VMEM((16, 128), jnp.int32),
            pltpu.VMEM((16, 128), jnp.int32),
            pltpu.VMEM((512, 2048), BF),
            pltpu.VMEM((1024, 128), BF),
            pltpu.VMEM((128, 2048), BF),
            pltpu.VMEM((4, 32, 128), F32),
            pltpu.VMEM((4, 32, 128), F32),
            pltpu.VMEM((4, 32, 128), F32),
            pltpu.VMEM((4, 32, 128), F32),
            pltpu.VMEM((128, 4096), BF),
            pltpu.VMEM((48, 4096), BF),
            pltpu.VMEM((256, 1024), BF),
            pltpu.VMEM((4, 2, 128, 128), F32),
            pltpu.VMEM((4, 128, 128), F32),
            pltpu.VMEM((32, 16, 128), F32),
            pltpu.VMEM((32, 16, 128), F32),
            dma((5,)), dma((4,)),
            dma, dma, dma, dma,
            dma((4,)), dma((4,)), dma, dma,
        ],
        compiler_params=pltpu.CompilerParams(
            collective_id=0, has_side_effects=True, vmem_limit_bytes=40 * 1024 * 1024
        ),
        name="top_merge",
    )(
        *(
            pltpu.with_memory_space_constraint(v, pltpu.HBM)
            for v in (
                eigen_slab.reshape(8, 4, 2, 16, 1024),
                secular_poles.reshape(16, 128),
                coupling.reshape(16, 128),
                window_roots.reshape(1, 128),
                deflated.reshape(16, 128),
                column_map.reshape(16, 128),
            )
        )
    )


def solution(mesh):
    return jax.shard_map(
        body,
        mesh=mesh,
        in_specs=(P("row", "col"), P("col"), P("col"), P(), P("col"), P("col")),
        out_specs=P(("row", "col"), None),
        check_vma=False,
    )
```

```python
import jax
import jax.numpy as jnp
from jax import lax
from jax.experimental import pallas as pl
from jax.experimental.pallas import tpu as pltpu
from jax.sharding import PartitionSpec as P

MESH = pl.DeviceIdType.MESH
BF = jnp.bfloat16
F32 = jnp.float32
NT = (((1,), (1,)), ((), ()))
HALF = 65536
STEPS_Z = (4, 3, 5, 2, 6, 1, 7, 0)
STEPS_X = (2, 1, 3, 0)


def dot_nt(a, b):
    return lax.dot_general(a, b, NT, preferred_element_type=F32)


def split3(v):
    hi = v.astype(BF)
    rest = v - hi.astype(F32)
    mid = rest.astype(BF)
    low = (rest - mid.astype(F32)).astype(BF)
    return hi.astype(F32), mid.astype(F32), low.astype(F32)


def kernel(
    slab, poles_in, coup_in, roots_in, defl_in, cmap_in, out_ref,
    sf, sh, sl, poles, coup, roots, defl, cmap,
    pieces, hots, slots, outgoing, recv_a,
    place_l, place_r, entry, prod, recv_c, send_r, recv_r,
    in_sem, slab_sem, sa, ra, sc, rc, sr, rr,
):
    row = lax.axis_index("row")
    col = lax.axis_index("col")
    chip = col // 2
    z = chip // 4
    x = chip % 4
    core = col % 2
    sibling = (row, chip * 2 + (1 - core))
    others = [
        lax.rem(z + dz, 8) * 4 + lax.rem(x + dx, 4) for dz in STEPS_Z for dx in STEPS_X if dz or dx
    ]

    smalls = [
        pltpu.make_async_copy(s, d, in_sem.at[i])
        for i, (s, d) in enumerate(
            [(cmap_in, cmap), (poles_in, poles), (coup_in, coup), (defl_in, defl), (roots_in, roots)]
        )
    ]
    for c in smalls:
        c.start()
    everyone = [to * 2 + c for to in others for c in (core, 1 - core)] + [chip * 2 + (1 - core)]
    barrier = pltpu.get_barrier_semaphore()
    for to in everyone:
        pl.semaphore_signal(barrier, inc=1, device_id=(row, to), device_id_type=MESH)

    slabs = [
        pltpu.make_async_copy(slab.at[:, i], sf.at[i], slab_sem.at[i]) for i in range(4)
    ]
    for c in slabs:
        c.start()

    for c in smalls:
        c.wait()

    cm = cmap[...]
    upper = (cm >= HALF).astype(jnp.int32)
    within = cm - upper * HALF
    target = within >> 10
    local = within & 1023
    order = jnp.where(upper == row // 4, target, -1)
    pole_v = poles[...]
    coup_v = jnp.where(defl[...] == 0, coup[...], 0.0)
    vals = (
        *split3(pole_v),
        *split3(coup_v),
        (local >> 7).astype(F32),
        (local & 127).astype(F32),
    )
    dest_id = lax.broadcasted_iota(jnp.int32, (64, 128), 0)
    slot_id = (lax.broadcasted_iota(jnp.int32, (128, 128), 0) & 63).astype(F32)
    for b in range(16):
        hots[pl.ds(64 * b, 64), :] = (order[b:b + 1, :] == dest_id).astype(F32).astype(BF)
    before = lax.broadcasted_iota(jnp.int32, (128, 256), 0)
    at = lax.broadcasted_iota(jnp.int32, (128, 256), 1)
    tri = ((before < at) | (at >= 128)).astype(F32).astype(BF)
    counts = jnp.dot(hots[...], tri, preferred_element_type=F32)
    carry = jnp.zeros((64, 128), F32)
    for b in range(16):
        lanes = pl.ds(128 * b, 128)
        hot = hots[pl.ds(64 * b, 64), :]
        block = counts[64 * b:64 * b + 64]
        rank = jnp.sum(hot.astype(F32) * (block[:, :128] + carry), axis=0, keepdims=True)
        carry = carry + block[:, 128:]
        slots[:, lanes] = (rank == slot_id).astype(F32).astype(BF)
        for i, v in enumerate(vals):
            pieces[pl.ds(64 * i, 64), lanes] = hot * jnp.broadcast_to(v[b:b + 1, :], (64, 128)).astype(BF)
    routed = dot_nt(pieces[...], slots[...])
    pole_o = (routed[0:64] + routed[64:128]) + routed[128:192]
    coup_o = (routed[192:256] + routed[256:320]) + routed[320:384]
    at_o = routed[384:448] * 128.0 + routed[448:512]
    roots_t = jnp.transpose(jnp.broadcast_to(roots[...], (128, 128)))
    sums = jnp.zeros((128, 128), F32)
    for b in range(16):
        e = coup_v[b:b + 1, :] / (pole_v[b:b + 1, :] - roots_t)
        sums = sums + e * e
    sums = jnp.sum(jnp.transpose(sums), axis=0, keepdims=True)
    low_lane = lax.broadcasted_iota(jnp.int32, (64, 128), 1) < 64
    outgoing[0] = jnp.where(low_lane, pole_o, coup_o)
    outgoing[1] = at_o
    outgoing[2] = jnp.broadcast_to(sums, (64, 128))

    pl.semaphore_wait(barrier, 63)
    for to in everyone:
        c = pltpu.make_async_remote_copy(
            src_ref=outgoing.at[:, pl.ds(to, 1)], dst_ref=recv_a.at[:, pl.ds(col, 1)],
            send_sem=sa, recv_sem=ra,
            device_id=(row, to), device_id_type=MESH,
        )
        c.start()

    for m in range(4):
        slabs[m].wait()
        for half in range(2):

            @pl.loop(0, 8)
            def _(q):
                v = sf[m, q // 4, q % 4, half]
                hi = v.astype(BF)
                at16 = pl.ds(pl.multiple_of(half * 128 + q * 16, 16), 16)
                sh[m, at16, :] = hi
                sl[m, at16, :] = (v - hi.astype(F32)).astype(BF)

    all_a = pltpu.make_async_remote_copy(
        src_ref=outgoing.at[:, pl.ds(0, 63)], dst_ref=recv_a.at[:, pl.ds(0, 63)],
        send_sem=sa, recv_sem=ra, device_id=sibling, device_id_type=MESH,
    )
    all_a.wait_recv()
    here = lax.broadcasted_iota(jnp.int32, (64, 128), 0) == col
    val, loc, sums = (jnp.where(here, outgoing[i], recv_a[i]) for i in range(3))
    scale = lax.rsqrt(jnp.sum(sums, axis=0, keepdims=True))

    low32 = lax.broadcasted_iota(jnp.int32, (32, 128), 1) < 64
    pole_r = jnp.where(low32, val[:32], pltpu.roll(val[32:], 64, 1))
    coup_r = jnp.where(low32, pltpu.roll(val[:32], 64, 1), val[32:])
    loc_r = jnp.where(low32, loc[:32], pltpu.roll(loc[32:], 64, 1)).astype(jnp.int32)
    loc_h = loc_r >> 7
    loc_l = loc_r & 127
    parts = (*split3(pole_r), *split3(coup_r))
    id128 = lax.broadcasted_iota(jnp.int32, (128, 128), 0)
    id8 = lax.broadcasted_iota(jnp.int32, (8, 128), 0)
    for b in range(32):
        lanes = pl.ds(128 * b, 128)
        place_l[:, lanes] = (loc_l[b:b + 1, :] == id128).astype(F32).astype(BF)
        hit = loc_h[b:b + 1, :] == id8
        place_r[:, lanes] = jnp.concatenate(
            [jnp.where(hit, v[b:b + 1, :], 0.0) for v in parts], axis=0
        ).astype(BF)
    placed = dot_nt(place_r[...], place_l[...])
    pole_p = (placed[0:8] + placed[8:16]) + placed[16:24]
    coup_p = (placed[24:32] + placed[32:40]) + placed[40:48]
    for h in range(8):
        e = coup_p[h:h + 1, :] / (pole_p[h:h + 1, :] - roots_t)
        hi = e.astype(BF)
        lanes = pl.ds(128 * h, 128)
        entry[pl.ds(0, 128), lanes] = hi
        entry[pl.ds(128, 128), lanes] = (e - hi.astype(F32)).astype(BF)

    copies_c = []
    copies_r = []

    def send_on(m):
        copies_c[m].wait_recv()
        both = (prod[m, core] + recv_c[m]).reshape(8, 16, 128)
        send_r[pl.ds(4 * m, 4)] = both[:4]
        send_r[pl.ds(4 * m + 16, 4)] = both[4:]
        for i in range(8):
            to = (m + i // 4 * 4) * 4 + lax.rem(x + STEPS_X[i % 4], 4)

            @pl.when(to != chip)
            def _():
                remote(to).start()

    def remote(to):
        return pltpu.make_async_remote_copy(
            src_ref=send_r.at[to], dst_ref=recv_r.at[chip], send_sem=sr, recv_sem=rr,
            device_id=(row, to * 2 + core), device_id_type=MESH,
        )

    for m in range(4):
        r1 = dot_nt(sh[m], entry[...])
        r2 = dot_nt(sl[m], entry[pl.ds(0, 128), :])
        p = (r1[:, 128:] + r2) + r1[:, :128]
        prod[m] = p.reshape(2, 128, 128)
        c = pltpu.make_async_remote_copy(
            src_ref=prod.at[m, 1 - core], dst_ref=recv_c.at[m], send_sem=sc.at[m], recv_sem=rc.at[m],
            device_id=sibling, device_id_type=MESH,
        )
        c.start()
        copies_c.append(c)
        if m:
            send_on(m - 1)
    send_on(3)
    all_r = pltpu.make_async_remote_copy(
        src_ref=send_r.at[pl.ds(0, 31)], dst_ref=recv_r.at[pl.ds(0, 31)],
        send_sem=sr, recv_sem=rr, device_id=sibling, device_id_type=MESH,
    )
    all_r.wait_recv()
    final = send_r[chip]
    for to in others:
        final = final + recv_r[to]
    out_ref[...] = final * scale
    for c in [all_a, all_r, *copies_c]:
        c.wait_send()


def body(eigen_slab, secular_poles, coupling, window_roots, deflated, column_map):
    hbm = pl.BlockSpec(memory_space=pltpu.HBM)
    dma = pltpu.SemaphoreType.DMA
    return pl.pallas_call(
        kernel,
        out_shape=jax.ShapeDtypeStruct((16, 128), F32),
        in_specs=[hbm] * 6,
        out_specs=pl.BlockSpec(memory_space=pltpu.VMEM),
        scratch_shapes=[
            pltpu.VMEM((4, 2, 4, 2, 16, 1024), F32),
            pltpu.VMEM((4, 256, 1024), BF),
            pltpu.VMEM((4, 256, 1024), BF),
            pltpu.VMEM((16, 128), F32),
            pltpu.VMEM((16, 128), F32),
            pltpu.VMEM((1, 128), F32),
            pltpu.VMEM((16, 128), jnp.int32),
            pltpu.VMEM((16, 128), jnp.int32),
            pltpu.VMEM((512, 2048), BF),
            pltpu.VMEM((1024, 128), BF),
            pltpu.VMEM((128, 2048), BF),
            pltpu.VMEM((3, 64, 128), F32),
            pltpu.VMEM((3, 64, 128), F32),
            pltpu.VMEM((128, 4096), BF),
            pltpu.VMEM((48, 4096), BF),
            pltpu.VMEM((256, 1024), BF),
            pltpu.VMEM((4, 2, 128, 128), F32),
            pltpu.VMEM((4, 128, 128), F32),
            pltpu.VMEM((32, 16, 128), F32),
            pltpu.VMEM((32, 16, 128), F32),
            dma((5,)), dma((4,)),
            dma, dma,
            dma((4,)), dma((4,)), dma, dma,
        ],
        compiler_params=pltpu.CompilerParams(
            collective_id=0, has_side_effects=True, vmem_limit_bytes=40 * 1024 * 1024
        ),
        name="top_merge",
    )(
        *(
            pltpu.with_memory_space_constraint(v, pltpu.HBM)
            for v in (
                eigen_slab.reshape(2, 4, 4, 2, 16, 1024),
                secular_poles.reshape(16, 128),
                coupling.reshape(16, 128),
                window_roots.reshape(1, 128),
                deflated.reshape(16, 128),
                column_map.reshape(16, 128),
            )
        )
    )


def solution(mesh):
    return jax.shard_map(
        body,
        mesh=mesh,
        in_specs=(P("row", "col"), P("col"), P("col"), P(), P("col"), P("col")),
        out_specs=P(("row", "col"), None),
        check_vma=False,
    )
```

```python
import jax
import jax.numpy as jnp
from jax import lax
from jax.experimental import pallas as pl
from jax.experimental.pallas import tpu as pltpu
from jax.sharding import PartitionSpec as P

MESH = pl.DeviceIdType.MESH
BF = jnp.bfloat16
F32 = jnp.float32
NT = (((1,), (1,)), ((), ()))
HALF = 65536
STEPS_Z = (4, 3, 5, 2, 6, 1, 7, 0)
STEPS_X = (2, 1, 3, 0)


def dot_nt(a, b):
    return lax.dot_general(a, b, NT, preferred_element_type=F32)


def split3(v):
    hi = v.astype(BF)
    rest = v - hi.astype(F32)
    mid = rest.astype(BF)
    low = (rest - mid.astype(F32)).astype(BF)
    return hi.astype(F32), mid.astype(F32), low.astype(F32)


def kernel(
    slab, poles_in, coup_in, roots_in, defl_in, cmap_in, out_ref,
    sf, sh, sl, poles, coup, roots, defl, cmap,
    pieces, hots, slots, outgoing, recv_a,
    place_l, place_r, entry, prod, recv_c, send_r, recv_r,
    in_sem, slab_sem, sa, ra, sc, rc, sr, rr,
):
    row = lax.axis_index("row")
    col = lax.axis_index("col")
    chip = col // 2
    z = chip // 4
    x = chip % 4
    core = col % 2
    sibling = (row, chip * 2 + (1 - core))
    others = [
        lax.rem(z + dz, 8) * 4 + lax.rem(x + dx, 4) for dz in STEPS_Z for dx in STEPS_X if dz or dx
    ]

    smalls = [
        pltpu.make_async_copy(s, d, in_sem.at[i])
        for i, (s, d) in enumerate(
            [(cmap_in, cmap), (poles_in, poles), (coup_in, coup), (defl_in, defl), (roots_in, roots)]
        )
    ]
    for c in smalls:
        c.start()
    everyone = [to * 2 + c for to in others for c in (core, 1 - core)] + [chip * 2 + (1 - core)]
    barrier = pltpu.get_barrier_semaphore()
    for to in everyone[:36]:
        pl.semaphore_signal(barrier, inc=1, device_id=(row, to), device_id_type=MESH)

    slabs = [
        pltpu.make_async_copy(slab.at[:, i], sf.at[i], slab_sem.at[i]) for i in range(4)
    ]
    for c in slabs:
        c.start()

    for c in smalls:
        c.wait()

    cm = cmap[...]
    upper = (cm >= HALF).astype(jnp.int32)
    within = cm - upper * HALF
    target = within >> 10
    local = within & 1023
    order = jnp.where(upper == row // 4, target, -1)
    pole_v = poles[...]
    coup_v = jnp.where(defl[...] == 0, coup[...], 0.0)
    vals = (
        *split3(pole_v),
        *split3(coup_v),
        (local >> 7).astype(F32),
        (local & 127).astype(F32),
    )
    dest_id = lax.broadcasted_iota(jnp.int32, (64, 128), 0)
    slot_id = (lax.broadcasted_iota(jnp.int32, (128, 128), 0) & 63).astype(F32)
    for b in range(16):
        hots[pl.ds(64 * b, 64), :] = (order[b:b + 1, :] == dest_id).astype(F32).astype(BF)
    before = lax.broadcasted_iota(jnp.int32, (128, 256), 0)
    at = lax.broadcasted_iota(jnp.int32, (128, 256), 1)
    tri = ((before < at) | (at >= 128)).astype(F32).astype(BF)
    counts = jnp.dot(hots[...], tri, preferred_element_type=F32)
    carry = jnp.zeros((64, 128), F32)
    for b in range(16):
        lanes = pl.ds(128 * b, 128)
        hot = hots[pl.ds(64 * b, 64), :]
        block = counts[64 * b:64 * b + 64]
        rank = jnp.sum(hot.astype(F32) * (block[:, :128] + carry), axis=0, keepdims=True)
        carry = carry + block[:, 128:]
        slots[:, lanes] = (rank == slot_id).astype(F32).astype(BF)
        for i, v in enumerate(vals):
            pieces[pl.ds(64 * i, 64), lanes] = hot * jnp.broadcast_to(v[b:b + 1, :], (64, 128)).astype(BF)
    routed = dot_nt(pieces[...], slots[...])
    pole_o = (routed[0:64] + routed[64:128]) + routed[128:192]
    coup_o = (routed[192:256] + routed[256:320]) + routed[320:384]
    at_o = routed[384:448] * 128.0 + routed[448:512]
    roots_t = jnp.transpose(jnp.broadcast_to(roots[...], (128, 128)))
    sums = jnp.zeros((128, 128), F32)
    for b in range(16):
        e = coup_v[b:b + 1, :] / (pole_v[b:b + 1, :] - roots_t)
        sums = sums + e * e
    sums = jnp.sum(jnp.transpose(sums), axis=0, keepdims=True)
    low_lane = lax.broadcasted_iota(jnp.int32, (64, 128), 1) < 64
    outgoing[0] = jnp.where(low_lane, pole_o, coup_o)
    outgoing[1] = at_o
    outgoing[2] = jnp.broadcast_to(sums, (64, 128))

    for to in everyone[36:]:
        pl.semaphore_signal(barrier, inc=1, device_id=(row, to), device_id_type=MESH)
    pl.semaphore_wait(barrier, 63)
    for to in everyone:
        c = pltpu.make_async_remote_copy(
            src_ref=outgoing.at[:, pl.ds(to, 1)], dst_ref=recv_a.at[:, pl.ds(col, 1)],
            send_sem=sa, recv_sem=ra,
            device_id=(row, to), device_id_type=MESH,
        )
        c.start()

    for m in range(4):
        slabs[m].wait()
        for half in range(2):

            @pl.loop(0, 8)
            def _(q):
                v = sf[m, q // 4, q % 4, half]
                hi = v.astype(BF)
                at16 = pl.ds(pl.multiple_of(half * 128 + q * 16, 16), 16)
                sh[m, at16, :] = hi
                sl[m, at16, :] = (v - hi.astype(F32)).astype(BF)

    all_a = pltpu.make_async_remote_copy(
        src_ref=outgoing.at[:, pl.ds(0, 63)], dst_ref=recv_a.at[:, pl.ds(0, 63)],
        send_sem=sa, recv_sem=ra, device_id=sibling, device_id_type=MESH,
    )
    all_a.wait_recv()
    here = lax.broadcasted_iota(jnp.int32, (64, 128), 0) == col
    val, loc, sums = (jnp.where(here, outgoing[i], recv_a[i]) for i in range(3))
    scale = lax.rsqrt(jnp.sum(sums, axis=0, keepdims=True))

    low32 = lax.broadcasted_iota(jnp.int32, (32, 128), 1) < 64
    pole_r = jnp.where(low32, val[:32], pltpu.roll(val[32:], 64, 1))
    coup_r = jnp.where(low32, pltpu.roll(val[:32], 64, 1), val[32:])
    loc_r = jnp.where(low32, loc[:32], pltpu.roll(loc[32:], 64, 1)).astype(jnp.int32)
    loc_h = loc_r >> 7
    loc_l = loc_r & 127
    parts = (*split3(pole_r), *split3(coup_r))
    id128 = lax.broadcasted_iota(jnp.int32, (128, 128), 0)
    id8 = lax.broadcasted_iota(jnp.int32, (8, 128), 0)
    for b in range(32):
        lanes = pl.ds(128 * b, 128)
        place_l[:, lanes] = (loc_l[b:b + 1, :] == id128).astype(F32).astype(BF)
        hit = loc_h[b:b + 1, :] == id8
        place_r[:, lanes] = jnp.concatenate(
            [jnp.where(hit, v[b:b + 1, :], 0.0) for v in parts], axis=0
        ).astype(BF)
    placed = dot_nt(place_r[...], place_l[...])
    pole_p = (placed[0:8] + placed[8:16]) + placed[16:24]
    coup_p = (placed[24:32] + placed[32:40]) + placed[40:48]
    for h in range(8):
        e = coup_p[h:h + 1, :] / (pole_p[h:h + 1, :] - roots_t)
        hi = e.astype(BF)
        lanes = pl.ds(128 * h, 128)
        entry[pl.ds(0, 128), lanes] = hi
        entry[pl.ds(128, 128), lanes] = (e - hi.astype(F32)).astype(BF)

    copies_c = []
    copies_r = []

    def send_on(m):
        copies_c[m].wait_recv()
        both = (prod[m, core] + recv_c[m]).reshape(8, 16, 128)
        send_r[pl.ds(4 * m, 4)] = both[:4]
        send_r[pl.ds(4 * m + 16, 4)] = both[4:]
        for i in range(8):
            to = (m + i // 4 * 4) * 4 + lax.rem(x + STEPS_X[i % 4], 4)

            if STEPS_X[i % 4]:
                remote(to).start()
            else:

                @pl.when(to != chip)
                def _():
                    remote(to).start()

    def remote(to):
        return pltpu.make_async_remote_copy(
            src_ref=send_r.at[to], dst_ref=recv_r.at[chip], send_sem=sr, recv_sem=rr,
            device_id=(row, to * 2 + core), device_id_type=MESH,
        )

    for m in range(4):
        r1 = dot_nt(sh[m], entry[...])
        r2 = dot_nt(sl[m], entry[pl.ds(0, 128), :])
        p = (r1[:, 128:] + r2) + r1[:, :128]
        prod[m] = p.reshape(2, 128, 128)
        c = pltpu.make_async_remote_copy(
            src_ref=prod.at[m, 1 - core], dst_ref=recv_c.at[m], send_sem=sc.at[m], recv_sem=rc.at[m],
            device_id=sibling, device_id_type=MESH,
        )
        c.start()
        copies_c.append(c)
        if m:
            send_on(m - 1)
    send_on(3)
    all_r = pltpu.make_async_remote_copy(
        src_ref=send_r.at[pl.ds(0, 31)], dst_ref=recv_r.at[pl.ds(0, 31)],
        send_sem=sr, recv_sem=rr, device_id=sibling, device_id_type=MESH,
    )
    all_r.wait_recv()
    final = send_r[chip]
    for to in others:
        final = final + recv_r[to]
    out_ref[...] = final * scale
    for c in [all_a, all_r, *copies_c]:
        c.wait_send()


def body(eigen_slab, secular_poles, coupling, window_roots, deflated, column_map):
    hbm = pl.BlockSpec(memory_space=pltpu.HBM)
    dma = pltpu.SemaphoreType.DMA
    return pl.pallas_call(
        kernel,
        out_shape=jax.ShapeDtypeStruct((16, 128), F32),
        in_specs=[hbm] * 6,
        out_specs=pl.BlockSpec(memory_space=pltpu.VMEM),
        scratch_shapes=[
            pltpu.VMEM((4, 2, 4, 2, 16, 1024), F32),
            pltpu.VMEM((4, 256, 1024), BF),
            pltpu.VMEM((4, 256, 1024), BF),
            pltpu.VMEM((16, 128), F32),
            pltpu.VMEM((16, 128), F32),
            pltpu.VMEM((1, 128), F32),
            pltpu.VMEM((16, 128), jnp.int32),
            pltpu.VMEM((16, 128), jnp.int32),
            pltpu.VMEM((512, 2048), BF),
            pltpu.VMEM((1024, 128), BF),
            pltpu.VMEM((128, 2048), BF),
            pltpu.VMEM((3, 64, 128), F32),
            pltpu.VMEM((3, 64, 128), F32),
            pltpu.VMEM((128, 4096), BF),
            pltpu.VMEM((48, 4096), BF),
            pltpu.VMEM((256, 1024), BF),
            pltpu.VMEM((4, 2, 128, 128), F32),
            pltpu.VMEM((4, 128, 128), F32),
            pltpu.VMEM((32, 16, 128), F32),
            pltpu.VMEM((32, 16, 128), F32),
            dma((5,)), dma((4,)),
            dma, dma,
            dma((4,)), dma((4,)), dma, dma,
        ],
        compiler_params=pltpu.CompilerParams(
            collective_id=0, has_side_effects=True, vmem_limit_bytes=40 * 1024 * 1024
        ),
        name="top_merge",
    )(
        *(
            pltpu.with_memory_space_constraint(v, pltpu.HBM)
            for v in (
                eigen_slab.reshape(2, 4, 4, 2, 16, 1024),
                secular_poles.reshape(16, 128),
                coupling.reshape(16, 128),
                window_roots.reshape(1, 128),
                deflated.reshape(16, 128),
                column_map.reshape(16, 128),
            )
        )
    )


def solution(mesh):
    return jax.shard_map(
        body,
        mesh=mesh,
        in_specs=(P("row", "col"), P("col"), P("col"), P(), P("col"), P("col")),
        out_specs=P(("row", "col"), None),
        check_vma=False,
    )
```
